256 devices in a mesh: grp: 4 (over x), dev: 64 (over y, z, core).
Axes of the slice: x: 4, y: 4, z: 8, core: 2. Of those that a mesh axis runs over, the one named last changes fastest.
Arguments:
- positions: float32 [3, 65536], P(None, ('grp', 'dev')), may hold values from -1 to 1
- velocities: float32 [3, 65536], P(None, ('grp', 'dev')), may hold values from -4 to 4
- accel_old: float32 [3, 65536], P(None, ('grp', 'dev')), may hold values from -6 to 6
- jerk_old: float32 [3, 65536], P(None, ('grp', 'dev')), may hold values from -6 to 6
- masses: float32 [65536], P(('grp', 'dev')), may hold values from 3.0517579e-06 to 7.6293945e-05
- levels: int32 [65536], P(('grp', 'dev')), may hold values from 0 to 3
- live_count: int32 [256], P(('grp', 'dev')), may hold values from 128 to 256, as said below
- active_slot: int32 [32768], P(('grp', 'dev')), may hold values from 0 to 255, as said below
Outputs:
- pos_vel: float32 [6, 32768], P(None, ('grp', 'dev'))
- acc_jerk: float32 [6, 32768], P(None, ('grp', 'dev'))
- potential: float32 [32768], P(('grp', 'dev'))
The draws below stay inside these ranges and needn't reach their ends.
Inputs may be any that keep to these rules, and one draw needn't show every extreme that they name: `live_count`: every entry is at least 128; some device is full with 256 and some has exactly 128; the counts are uneven across devices. `active_slot`: within each device's aligned block of 128 entries the slots are distinct and below that device's live_count.
All inputs are finite; a program needn't handle non-finite values.
Results may differ from the reference program's by a relative error of at most 0.00029.
Values sent between devices are 32-bit elements; how exact they have to be, the bound alone decides.
No kernel may reach another device: no remote copies, remote signals or barrier semaphores. Data moves between devices by JAX's collectives and lax.ppermute only.
A program may use at most 64 MiB of HBM per device.

```python
import math
import jax
import jax.numpy as jnp
from jax import lax

SRC_DEV = 256
ACT_DEV = 128
LEVELS = 4
SOURCES = 65536
NACT = 32768
DEVICES = 256


def live_counts_helper(key):
    base = jax.random.fold_in(key, 11)
    roll = jax.random.randint(base, (DEVICES,), 0, 33)
    counts = ACT_DEV + (SRC_DEV - ACT_DEV) * roll * roll // 1024
    full_device = jax.random.randint(jax.random.fold_in(key, 12), (), 0, DEVICES)
    counts = counts.at[full_device].set(SRC_DEV)
    counts = counts.at[(full_device + 1) % DEVICES].set(ACT_DEV)
    return counts.astype(jnp.int32)


def draw_live_count(key, part):
    return live_counts_helper(key)


def draw_active_slot(key, part):
    counts = live_counts_helper(key)
    column = jnp.arange(SRC_DEV, dtype=jnp.int32)[None, :]
    scores = jax.random.randint(jax.random.fold_in(key, 13), (DEVICES, SRC_DEV), 0, 2 ** 19) * SRC_DEV + column
    scores = scores + (column >= counts[:, None]).astype(jnp.int32) * 2 ** 30
    first = (column == SRC_DEV - 1) & (counts[:, None] == SRC_DEV)
    scores = jnp.where(first, -1, scores)
    order = jnp.argsort(scores, axis=1, stable=True)[:, :ACT_DEV]
    return order.reshape(-1).astype(jnp.int32)


def touch_ends(array, stream_key, smallest, largest):
    longest = array.shape.index(max(array.shape))
    spots = []
    for shift in (0, 1):
        where = [jax.random.randint(jax.random.fold_in(stream_key, axis), (), 0, length) for axis, length in enumerate(array.shape)]
        where[longest] = (where[longest] + shift) % array.shape[longest]
        spots.append(tuple(where))
    return array.at[spots[0]].set(smallest).at[spots[1]].set(largest)


def shard_levels(stream_key, extent, split, smallest, high):
    def one(position, blocks):
        heights = jax.random.uniform(jax.random.fold_in(jax.random.fold_in(stream_key, 6), position), (blocks,), jnp.float32, smallest / len(split), high / len(split))
        return jnp.repeat(jnp.exp(heights), extent[position] // blocks).reshape((-1,) + (1,) * (len(extent) - position - 1))

    gain = one(*split[0])
    for cut in split[1:]:
        gain = gain * one(*cut)
    return gain


def centred(key, dims, deviation, limit, cuts=(), kind=jnp.bfloat16):
    gain = shard_levels(key, dims, cuts, -0.22, 0.18) if cuts else 1.0
    drawn = jax.random.normal(key, dims, jnp.float32) * deviation * gain
    return jnp.minimum(jnp.maximum(drawn, -limit), limit).astype(kind)


def setup_inputs(seed: int = 0) -> dict:
    keys = jax.random.split(jax.random.key(seed), 9)
    return {
        "positions": jnp.clip(jax.random.uniform(keys[0], (3, SOURCES), jnp.float32, -1.0, 1.0) * shard_levels(keys[0], (3, SOURCES), ((1, 256),), -0.4, 0.0), -1.0, 1.0),
        "velocities": centred(keys[1], (3, SOURCES), 0.5, 4.0, ((1, 256),), jnp.float32),
        "accel_old": centred(keys[2], (3, SOURCES), 1.0, 6.0, ((1, 256),), jnp.float32),
        "jerk_old": centred(keys[3], (3, SOURCES), 1.0, 6.0, ((1, 256),), jnp.float32),
        "masses": jnp.clip(jnp.exp(math.log(7.62939453125e-05) - 3.218876 * jax.random.uniform(keys[4], (SOURCES,), jnp.float32) ** shard_levels(keys[4], (SOURCES,), ((0, 256),), -0.2, 0.2)), 3.051757857974735e-06, 7.62939453125e-05),
        "levels": touch_ends(jax.random.randint(keys[5], (SOURCES,), 0, LEVELS), jax.random.fold_in(keys[5], 1), 0, LEVELS - 1).astype(jnp.int32),
        "live_count": draw_live_count(jax.random.fold_in(keys[8], 71), 0),
        "active_slot": draw_active_slot(jax.random.fold_in(keys[8], 71), 0),
    }


tau_base = 0.5
soften_sq = 0.0001

def pair_terms(active_state, src_pos, src_vel, src_mass):
    delta_pos = src_pos[:, None, :] - active_state[0:3, :, None]
    delta_vel = src_vel[:, None, :] - active_state[3:6, :, None]
    dist_sq = lax.optimization_barrier(jnp.sum(delta_pos * delta_pos, axis=0)) + soften_sq
    weight = src_mass[None, :] / jnp.sqrt(dist_sq)
    cubed = weight / dist_sq
    radial = 3.0 * lax.optimization_barrier(jnp.sum(delta_pos * delta_vel, axis=0)) / dist_sq
    accel = lax.optimization_barrier(jnp.sum(cubed[None] * delta_pos, axis=2))
    jerk_new = lax.optimization_barrier(jnp.sum(cubed[None] * (delta_vel - radial[None] * delta_pos), axis=2))
    pot_sum = -lax.optimization_barrier(jnp.sum(weight, axis=1))
    return jnp.concatenate([accel, jerk_new, pot_sum[None]], axis=0)

def correct(state, summed):
    pos_now = state[0:3]
    vel_now = state[3:6]
    acc_start = state[6:9]
    jerk_start = state[9:12]
    step_size = state[12:13]
    acc_end = summed[0:3]
    jerk_end = summed[3:6]
    differ = acc_start - acc_end
    fourth = -6.0 * differ - step_size * (4.0 * jerk_start + 2.0 * jerk_end)
    fifth = 12.0 * differ + 6.0 * step_size * (jerk_start + jerk_end)
    new_pos = pos_now + step_size * step_size / 24.0 * fourth + step_size * step_size / 120.0 * fifth
    new_vel = vel_now + step_size / 6.0 * fourth + step_size / 24.0 * fifth
    return (jnp.concatenate([new_pos, new_vel], axis=0), summed[0:6], summed[6])

def reference(positions, velocities, accel_old, jerk_old, masses, levels, live_count, active_slot):
    elapsed = tau_base * jnp.exp2(-levels.astype(jnp.float32))
    pos_pred = positions + elapsed * (velocities + elapsed * (accel_old / 2.0 + elapsed * jerk_old / 6.0))
    vel_pred = velocities + elapsed * (accel_old + elapsed * jerk_old / 2.0)
    indices = jnp.arange(SOURCES, dtype=jnp.int32)
    owner = indices // SRC_DEV
    live = indices % SRC_DEV < live_count[owner]
    live_mass = jnp.where(live, masses, jnp.float32(0.0))
    star = jnp.arange(NACT, dtype=jnp.int32) // ACT_DEV * SRC_DEV + active_slot
    state = jnp.concatenate([pos_pred[:, star], vel_pred[:, star], accel_old[:, star], jerk_old[:, star], elapsed[star][None]], axis=0)
    block_size = min(128, NACT)
    blocks = state[0:6].reshape(6, NACT // block_size, block_size).transpose(1, 0, 2)
    summed = lax.map(lambda blk: pair_terms(blk, pos_pred, vel_pred, live_mass), blocks)
    summed = summed.transpose(1, 0, 2).reshape(7, NACT)
    return correct(state, summed)
```

```python
import functools
import jax
import jax.numpy as jnp
from jax import lax
from jax.experimental import pallas as pl
from jax.experimental.pallas import tpu as pltpu
from jax.sharding import Mesh, PartitionSpec as P

soften_sq = 0.0001
BF = jnp.bfloat16
F32 = jnp.float32


def round_bf(x):
    return x.astype(BF).astype(F32)


def pieces3(x):
    a = round_bf(x)
    r = x - a
    b = round_bf(r)
    return a, b, round_bf(r - b)


def row_ids(shape):
    return lax.broadcasted_iota(jnp.int32, shape, 0)


def grid_split(x):
    row = row_ids(x.shape)
    x = jnp.where(row < 6, x, 0.0)
    up = jnp.where(row < 3, 64.0, 32.0)
    down = jnp.where(row < 3, 1.0 / 64.0, 1.0 / 32.0)
    coarse = jnp.round(x * up) * down
    rest = x - coarse
    p1 = round_bf(rest)
    p2 = round_bf(rest - p1)
    return coarse, p1, p2


def stack_scalar(first, second, swapped):
    n = first.shape[1]
    one = jnp.ones((1, n), F32)
    zero = jnp.zeros((2, n), F32)
    a = pieces3(first)
    if swapped:
        return jnp.concatenate([one, one, one, *a, zero], axis=0)
    return jnp.concatenate([*a, one, one, one, zero], axis=0)


def scalars(coarse, p1, p2):
    fine = p1 + p2
    h, l = coarse[0:3], fine[0:3]
    vh, vl = coarse[3:6], fine[3:6]
    norm_exact = jnp.sum(h * h, axis=0, keepdims=True)
    norm_rest = jnp.sum(2.0 * h * l + l * l, axis=0, keepdims=True)
    dot_exact = jnp.sum(h * vh, axis=0, keepdims=True)
    dot_rest = jnp.sum(h * vl + l * vh + l * vl, axis=0, keepdims=True)
    return norm_exact, norm_rest, dot_exact, dot_rest


def source_features(x):
    c, p1, p2 = grid_split(x)
    ne, nr, de, dr = scalars(c, p1, p2)
    n = x.shape[1]
    s = [stack_scalar(v, None, False) for v in (ne, de, nr, dr)]
    zero = jnp.zeros((8, n), F32)
    return jnp.concatenate([s[0], s[1], c, p1, p2, c, c, p1, p2, p1, s[2], s[3], zero, zero, zero, zero], axis=0)


def active_features(x):
    c, p1, p2 = grid_split(x)
    ne, nr, de, dr = scalars(c, p1, p2)
    n = x.shape[1]
    row = row_ids(x.shape)

    def norm_side(t):
        return jnp.where(row < 3, -2.0 * t, 0.0)

    def dot_side(t):
        return jnp.concatenate([-t[3:6], -t[0:3], t[6:8]], axis=0)

    zero = jnp.zeros((8, n), F32)

    def build(side, exact, rest, is_norm):
        se = stack_scalar(exact, None, True)
        sr = stack_scalar(rest, None, True)
        first = [se, zero] if is_norm else [zero, se]
        last = [sr, zero] if is_norm else [zero, sr]
        h, a, b = side(c), side(p1), side(p2)
        return jnp.concatenate([*first, h, h, h, a, b, a, a, b, *last, zero, zero, zero, zero], axis=0)

    return build(norm_side, ne, nr + soften_sq, True), build(dot_side, de, dr, False)


def reduce_rows(x):
    row = row_ids(x.shape)
    mass = x[6:7]
    y = jnp.where(row < 6, x, jnp.where(row == 6, 1.0, 0.0)) * mass
    a, b, c = pieces3(y)
    return jnp.concatenate([a, b, c, jnp.zeros_like(a)], axis=0)


def split_hi_lo(t):
    hi = t.astype(BF)
    return hi, (t - hi.astype(F32)).astype(BF)


def pair_kernel(n_src, n_act, act_ref, src_ref, out_ref, dense, feat_j, feat_q, feat_d, red_ref, acc_u, acc_p, acc_w):
    tile = 256
    total_act = n_act * 128
    width = n_src * 256 + 512
    for t in range(width // 128):
        dense[:, t * 128:(t + 1) * 128] = jnp.zeros((8, 128), F32)
    lane = lax.broadcasted_iota(jnp.int32, (8, 128), 1)
    counts = [jnp.max(src_ref[b, 7:8, 0:128]).astype(jnp.int32) for b in range(n_src)]
    offset = jnp.int32(0)
    for b in range(n_src):
        shift = lax.rem(offset, 128)
        start = pl.multiple_of(offset - shift, 128)
        left = pltpu.roll(src_ref[b, :, 0:128], shift, 1)
        right = pltpu.roll(src_ref[b, :, 128:256], shift, 1)
        before = lane < shift
        dense[:, pl.ds(start, 128)] = jnp.where(before, dense[:, pl.ds(start, 128)], left)
        dense[:, pl.ds(start + 128, 128)] = jnp.where(before, left, right)
        dense[:, pl.ds(start + 256, 128)] = jnp.where(before, right, 0.0)
        offset = offset + counts[b]
    n_blocks = (offset + (tile - 1)) // tile
    for k in range(n_act):
        fq, fd = active_features(act_ref[k])
        feat_q[:, k * 128:(k + 1) * 128] = fq.astype(BF)
        feat_d[:, k * 128:(k + 1) * 128] = fd.astype(BF)
    acc_u[...] = jnp.zeros_like(acc_u)
    acc_p[...] = jnp.zeros_like(acc_p)
    acc_w[...] = jnp.zeros_like(acc_w)

    def block(b, _):
        x = dense[:, pl.ds(pl.multiple_of(b * tile, tile), tile)]
        feat_j[...] = source_features(x).T.astype(BF)
        red_ref[...] = reduce_rows(x).astype(BF)

        def tiles(i, _):
            lanes = pl.ds(pl.multiple_of(i * tile, tile), tile)
            fj = feat_j[...]
            q = jnp.dot(fj, feat_q[:, lanes], preferred_element_type=F32)
            d = jnp.dot(fj, feat_d[:, lanes], preferred_element_type=F32)
            s = lax.rsqrt(q)
            s2 = s * s
            u = s * s2
            p = (u * s2) * d
            u_hi, u_lo = split_hi_lo(u)
            p_hi, p_lo = split_hi_lo(p)
            w = s.astype(BF)
            rows = red_ref[...]
            two = rows[0:16]
            def mm(a, b):
                return jnp.dot(a, b, preferred_element_type=F32)
            ru = mm(rows, u_hi)
            rp = mm(rows, p_hi)
            rul = mm(two, u_lo)
            rpl = mm(two, p_lo)
            rw = mm(two, w)
            acc_u[:, lanes] += (ru[0:8] + ru[8:16]) + (ru[16:24] + (rul[0:8] + rul[8:16]))
            acc_p[:, lanes] += (rp[0:8] + rp[8:16]) + (rp[16:24] + (rpl[0:8] + rpl[8:16]))
            acc_w[:, lanes] += rw[0:8] + rw[8:16]
            return 0

        lax.fori_loop(0, total_act // tile, tiles, 0)
        return 0

    lax.fori_loop(0, n_blocks, block, 0)
    for k in range(n_act):
        lanes = slice(k * 128, (k + 1) * 128)
        su = acc_u[:, lanes]
        sp = acc_p[:, lanes]
        sw = acc_w[:, lanes]
        st = act_ref[k]
        accel = su[0:3] - st[0:3] * su[6:7]
        jerk = su[3:6] - st[3:6] * su[6:7] - 3.0 * (sp[0:3] - st[0:3] * sp[6:7])
        out_ref[k] = jnp.concatenate([accel, jerk, -sw[6:7], jnp.zeros((1, 128), F32)], axis=0)


def pair_sums(actives, sources):
    n_act, n_src = actives.shape[0], sources.shape[0]
    total = n_act * 128
    return pl.pallas_call(
        functools.partial(pair_kernel, n_src, n_act),
        out_shape=jax.ShapeDtypeStruct((n_act, 8, 128), F32),
        in_specs=[pl.BlockSpec(memory_space=pltpu.VMEM)] * 2,
        out_specs=pl.BlockSpec(memory_space=pltpu.VMEM),
        scratch_shapes=[
            pltpu.VMEM((8, n_src * 256 + 512), F32),
            pltpu.VMEM((256, 128), BF),
            pltpu.VMEM((128, total), BF),
            pltpu.VMEM((128, total), BF),
            pltpu.VMEM((32, 256), BF),
            pltpu.VMEM((8, total), F32),
            pltpu.VMEM((8, total), F32),
            pltpu.VMEM((8, total), F32),
        ],
        name="pair_sums",
        cost_estimate=pl.CostEstimate(flops=400_000_000, bytes_accessed=400_000, transcendentals=8_000_000),
    )(actives, sources)


def pick(table, slot):
    rows = []
    for k in range(table.shape[0] // 8):
        part = table[8 * k:8 * k + 8]
        low = jnp.broadcast_to(lax.rem(slot, 128), (8, 128))
        left = jnp.take_along_axis(part[:, 0:128], low, axis=1)
        right = jnp.take_along_axis(part[:, 128:256], low, axis=1)
        rows.append(jnp.where(slot < 128, left, right))
    return jnp.concatenate(rows, axis=0)


def predict_kernel(pos_ref, vel_ref, acc_ref, jerk_ref, mass_ref, level_ref, live_ref, slot_ref, src_ref, own_ref, act_ref):
    level = level_ref[...]
    half = jnp.where((level & 1) == 1, 0.5, 1.0)
    h = 0.5 * half * jnp.where((level & 2) == 2, 0.25, 1.0)
    acc, jerk, vel = acc_ref[...], jerk_ref[...], vel_ref[...]
    pos_pred = pos_ref[...] + h * (vel + h * (acc / 2.0 + h * jerk / 6.0))
    vel_pred = vel + h * (acc + h * jerk / 2.0)
    slots = lax.broadcasted_iota(jnp.int32, (1, 256), 1)
    count = live_ref[0]
    mass = jnp.where(slots < count, mass_ref[...], 0.0)
    counts = jnp.full((1, 256), count, jnp.int32).astype(F32)
    src = jnp.concatenate([pos_pred, vel_pred, mass, counts], axis=0)
    for k in range(src_ref.shape[0]):
        src_ref[k] = src
    rest = jnp.concatenate([acc, jerk, h, h], axis=0)
    own = pick(jnp.concatenate([src, rest], axis=0), slot_ref[...])
    own_ref[...] = own
    for k in range(act_ref.shape[0]):
        act_ref[k] = own[0:8]


def correct_kernel(own_ref, part_ref, state_ref, deriv_ref, pot_ref):
    summed = part_ref[0]
    for k in range(1, part_ref.shape[0]):
        summed = summed + part_ref[k]
    own = own_ref[...]
    pos_now, vel_now = own[0:3], own[3:6]
    acc_start, jerk_start, step = own[8:11], own[11:14], own[14:15]
    acc_end, jerk_end = summed[0:3], summed[3:6]
    differ = acc_start - acc_end
    fourth = -6.0 * differ - step * (4.0 * jerk_start + 2.0 * jerk_end)
    fifth = 12.0 * differ + 6.0 * step * (jerk_start + jerk_end)
    new_pos = pos_now + step * step / 24.0 * fourth + step * step / 120.0 * fifth
    new_vel = vel_now + step / 6.0 * fourth + step / 24.0 * fifth
    state_ref[...] = jnp.concatenate([new_pos, new_vel], axis=0)
    deriv_ref[...] = summed[0:6]
    pot_ref[...] = summed[6:7]


VM = pl.BlockSpec(memory_space=pltpu.VMEM)
SM = pl.BlockSpec(memory_space=pltpu.SMEM)
SRC_AXES = ("y", "z")
ACT_AXES = ("x", "c")


def shards(positions, velocities, accel_old, jerk_old, masses, levels, live_count, active_slot):
    n_src, n_act = 32, 8
    src, own, act = pl.pallas_call(
        predict_kernel,
        out_shape=(
            jax.ShapeDtypeStruct((n_src, 8, 256), F32),
            jax.ShapeDtypeStruct((16, 128), F32),
            jax.ShapeDtypeStruct((n_act, 8, 128), F32),
        ),
        in_specs=[VM, VM, VM, VM, VM, VM, SM, VM],
        out_specs=(VM, VM, VM),
        name="predict",
    )(positions, velocities, accel_old, jerk_old, masses[None], levels[None], live_count, active_slot[None])
    actives = lax.all_to_all(act, ACT_AXES, 0, 0)
    sources = lax.all_to_all(src, SRC_AXES, 0, 0)
    partial_sums = pair_sums(actives, sources)
    parts = lax.all_to_all(partial_sums, ACT_AXES, 0, 0)
    state, deriv, pot = pl.pallas_call(
        correct_kernel,
        out_shape=(
            jax.ShapeDtypeStruct((6, 128), F32),
            jax.ShapeDtypeStruct((6, 128), F32),
            jax.ShapeDtypeStruct((1, 128), F32),
        ),
        in_specs=[VM, VM],
        out_specs=(VM, VM, VM),
        name="correct",
    )(own, parts)
    return state, deriv, pot[0]


def solution(mesh):
    fine = Mesh(mesh.devices.reshape(4, 4, 8, 2), ("x", "y", "z", "c"))
    every = ("x", "y", "z", "c")
    rows, flat = P(None, every), P(every)
    return jax.shard_map(
        shards,
        mesh=fine,
        in_specs=(rows, rows, rows, rows, flat, flat, flat, flat),
        out_specs=(rows, rows, flat),
        check_vma=False,
    )
```

```python
import functools
import jax
import jax.numpy as jnp
from jax import lax
from jax.experimental import pallas as pl
from jax.experimental.pallas import tpu as pltpu
from jax.sharding import Mesh, PartitionSpec as P

soften_sq = 0.0001
BF = jnp.bfloat16
F32 = jnp.float32


def round_bf(x):
    return x.astype(BF).astype(F32)


def pieces3(x):
    a = round_bf(x)
    r = x - a
    b = round_bf(r)
    return a, b, round_bf(r - b)


def row_ids(shape):
    return lax.broadcasted_iota(jnp.int32, shape, 0)


def grid_split(x):
    row = row_ids(x.shape)
    x = jnp.where(row < 6, x, 0.0)
    up = jnp.where(row < 3, 64.0, 32.0)
    down = jnp.where(row < 3, 1.0 / 64.0, 1.0 / 32.0)
    coarse = jnp.round(x * up) * down
    rest = x - coarse
    p1 = round_bf(rest)
    p2 = round_bf(rest - p1)
    return coarse, p1, p2


def stack_scalar(first, second, swapped):
    n = first.shape[1]
    one = jnp.ones((1, n), F32)
    zero = jnp.zeros((2, n), F32)
    a = pieces3(first)
    if swapped:
        return jnp.concatenate([one, one, one, *a, zero], axis=0)
    return jnp.concatenate([*a, one, one, one, zero], axis=0)


def scalars(coarse, p1, p2):
    fine = p1 + p2
    h, l = coarse[0:3], fine[0:3]
    vh, vl = coarse[3:6], fine[3:6]
    norm_exact = jnp.sum(h * h, axis=0, keepdims=True)
    norm_rest = jnp.sum(2.0 * h * l + l * l, axis=0, keepdims=True)
    dot_exact = jnp.sum(h * vh, axis=0, keepdims=True)
    dot_rest = jnp.sum(h * vl + l * vh + l * vl, axis=0, keepdims=True)
    return norm_exact, norm_rest, dot_exact, dot_rest


def source_features(x):
    c, p1, p2 = grid_split(x)
    ne, nr, de, dr = scalars(c, p1, p2)
    n = x.shape[1]
    s = [stack_scalar(v, None, False) for v in (ne, de, nr, dr)]
    zero = jnp.zeros((8, n), F32)
    return jnp.concatenate([s[0], s[1], c, p1, p2, c, c, p1, p2, p1, s[2], s[3], zero, zero, zero, zero], axis=0)


def active_features(x):
    c, p1, p2 = grid_split(x)
    ne, nr, de, dr = scalars(c, p1, p2)
    n = x.shape[1]
    row = row_ids(x.shape)

    def norm_side(t):
        return jnp.where(row < 3, -2.0 * t, 0.0)

    def dot_side(t):
        return jnp.concatenate([-t[3:6], -t[0:3], t[6:8]], axis=0)

    zero = jnp.zeros((8, n), F32)

    def build(side, exact, rest, is_norm):
        se = stack_scalar(exact, None, True)
        sr = stack_scalar(rest, None, True)
        first = [se, zero] if is_norm else [zero, se]
        last = [sr, zero] if is_norm else [zero, sr]
        h, a, b = side(c), side(p1), side(p2)
        return jnp.concatenate([*first, h, h, h, a, b, a, a, b, *last, zero, zero, zero, zero], axis=0)

    return build(norm_side, ne, nr + soften_sq, True), build(dot_side, de, dr, False)


def reduce_rows(x):
    row = row_ids(x.shape)
    mass = x[6:7]
    y = jnp.where(row < 6, x, jnp.where(row == 6, 1.0, 0.0)) * mass
    a, b, c = pieces3(y)
    return jnp.concatenate([a, b, c, jnp.zeros_like(a)], axis=0)


def split_hi_lo(t):
    hi = t.astype(BF)
    return hi, (t - hi.astype(F32)).astype(BF)


def pair_kernel(n_src, n_act, act_ref, src_ref, out_ref, dense, feat_j, feat_q, feat_d, red_ref, acc_u, acc_p, acc_w, *bufs):
    tile = 256
    n_tiles = n_act * 128 // tile
    q_bufs, d_bufs = bufs[0:2], bufs[2:4]
    v_bufs = bufs[4:6]
    width = n_src * 256 + 512
    for t in range(width // 128):
        dense[:, t * 128:(t + 1) * 128] = jnp.zeros((8, 128), F32)
    lane = lax.broadcasted_iota(jnp.int32, (8, 128), 1)
    counts = [jnp.max(src_ref[b, 7:8, 0:128]).astype(jnp.int32) for b in range(n_src)]
    offset = jnp.int32(0)
    for b in range(n_src):
        shift = lax.rem(offset, 128)
        start = pl.multiple_of(offset - shift, 128)
        left = pltpu.roll(src_ref[b, :, 0:128], shift, 1)
        right = pltpu.roll(src_ref[b, :, 128:256], shift, 1)
        before = lane < shift
        dense[:, pl.ds(start, 128)] = jnp.where(before, dense[:, pl.ds(start, 128)], left)
        dense[:, pl.ds(start + 128, 128)] = jnp.where(before, left, right)
        dense[:, pl.ds(start + 256, 128)] = jnp.where(before, right, 0.0)
        offset = offset + counts[b]
    n_pairs = (offset + (2 * tile - 1)) // (2 * tile)
    for k in range(n_act):
        fq, fd = active_features(act_ref[k])
        feat_q[k] = fq.astype(BF)
        feat_d[k] = fd.astype(BF)
    acc_u[...] = jnp.zeros_like(acc_u)
    acc_p[...] = jnp.zeros_like(acc_p)
    acc_w[...] = jnp.zeros_like(acc_w)
    red_ref[...] = jnp.zeros_like(red_ref)
    v_bufs[1][...] = jnp.zeros_like(v_bufs[1])

    def sources(b):
        return dense[:, pl.ds(pl.multiple_of(b * tile, tile), tile)]

    def wide(ref, *at):
        return jnp.concatenate([ref[(*at, 0)], ref[(*at, 1)]], axis=1)

    def generate(i):
        fj = feat_j[...]
        fq = jnp.concatenate([feat_q[2 * i], feat_q[2 * i + 1]], axis=1)
        fd = jnp.concatenate([feat_d[2 * i], feat_d[2 * i + 1]], axis=1)
        q_bufs[i % 2][...] = jnp.dot(fj, fq, preferred_element_type=F32)
        d_bufs[i % 2][...] = jnp.dot(fj, fd, preferred_element_type=F32)

    def combine(i):
        v = v_bufs[i % 2]
        for half in range(2):
            lanes = slice(half * 128, half * 128 + 128)
            q = q_bufs[i % 2][:, lanes]
            d = d_bufs[i % 2][:, lanes]
            s = lax.rsqrt(q)
            s2 = s * s
            u = s * s2
            p = (u * s2) * d
            v[0, half], v[1, half] = split_hi_lo(u)
            v[2, half], v[3, half] = split_hi_lo(p)
            v[4, half] = s.astype(BF)

    def reduce(i):
        v = v_bufs[i % 2]
        lanes = slice(i * tile, (i + 1) * tile)
        rows = red_ref[...]
        two = rows[0:16]

        def mm(a, k):
            return jnp.dot(a, wide(v, k), preferred_element_type=F32)

        ru, rul, rp, rpl, rw = mm(rows, 0), mm(two, 1), mm(rows, 2), mm(two, 3), mm(two, 4)
        acc_u[:, lanes] += (ru[0:8] + ru[8:16]) + (ru[16:24] + (rul[0:8] + rul[8:16]))
        acc_p[:, lanes] += (rp[0:8] + rp[8:16]) + (rp[16:24] + (rpl[0:8] + rpl[8:16]))
        acc_w[:, lanes] += rw[0:8] + rw[8:16]

    feat_j[...] = source_features(sources(0)).T.astype(BF)
    generate(0)

    def pair(k, _):
        for b in (2 * k, 2 * k + 1):
            fresh = source_features(sources(b + 1)).T.astype(BF)
            for i in range(n_tiles):
                if i == n_tiles - 1:
                    feat_j[...] = fresh
                generate((i + 1) % n_tiles)
                combine(i)
                reduce((i - 1) % n_tiles)
                if i == 0:
                    red_ref[...] = reduce_rows(sources(b)).astype(BF)
        return 0

    lax.fori_loop(0, n_pairs, pair, 0)
    reduce(n_tiles - 1)
    for k in range(n_act):
        lanes = slice(k * 128, (k + 1) * 128)
        su = acc_u[:, lanes]
        sp = acc_p[:, lanes]
        sw = acc_w[:, lanes]
        st = act_ref[k]
        accel = su[0:3] - st[0:3] * su[6:7]
        jerk = su[3:6] - st[3:6] * su[6:7] - 3.0 * (sp[0:3] - st[0:3] * sp[6:7])
        out_ref[k] = jnp.concatenate([accel, jerk, -sw[6:7], jnp.zeros((1, 128), F32)], axis=0)


def pair_sums(actives, sources):
    n_act, n_src = actives.shape[0], sources.shape[0]
    total = n_act * 128
    return pl.pallas_call(
        functools.partial(pair_kernel, n_src, n_act),
        out_shape=jax.ShapeDtypeStruct((n_act, 8, 128), F32),
        in_specs=[pl.BlockSpec(memory_space=pltpu.VMEM)] * 2,
        out_specs=pl.BlockSpec(memory_space=pltpu.VMEM),
        scratch_shapes=[
            pltpu.VMEM((8, n_src * 256 + 512), F32),
            pltpu.VMEM((256, 128), BF),
            pltpu.VMEM((n_act, 128, 128), BF),
            pltpu.VMEM((n_act, 128, 128), BF),
            pltpu.VMEM((32, 256), BF),
            pltpu.VMEM((8, total), F32),
            pltpu.VMEM((8, total), F32),
            pltpu.VMEM((8, total), F32),
            *[pltpu.VMEM((256, 256), F32) for _ in range(4)],
            *[pltpu.VMEM((5, 2, 256, 128), BF) for _ in range(2)],
        ],
        name="pair_sums",
        cost_estimate=pl.CostEstimate(flops=400_000_000, bytes_accessed=400_000, transcendentals=8_000_000),
    )(actives, sources)


def pick(table, slot):
    rows = []
    for k in range(table.shape[0] // 8):
        part = table[8 * k:8 * k + 8]
        low = jnp.broadcast_to(lax.rem(slot, 128), (8, 128))
        left = jnp.take_along_axis(part[:, 0:128], low, axis=1)
        right = jnp.take_along_axis(part[:, 128:256], low, axis=1)
        rows.append(jnp.where(slot < 128, left, right))
    return jnp.concatenate(rows, axis=0)


def predict_kernel(pos_ref, vel_ref, acc_ref, jerk_ref, mass_ref, level_ref, live_ref, slot_ref, src_ref, own_ref, act_ref):
    level = level_ref[...]
    half = jnp.where((level & 1) == 1, 0.5, 1.0)
    h = 0.5 * half * jnp.where((level & 2) == 2, 0.25, 1.0)
    acc, jerk, vel = acc_ref[...], jerk_ref[...], vel_ref[...]
    pos_pred = pos_ref[...] + h * (vel + h * (acc / 2.0 + h * jerk / 6.0))
    vel_pred = vel + h * (acc + h * jerk / 2.0)
    slots = lax.broadcasted_iota(jnp.int32, (1, 256), 1)
    count = live_ref[0]
    mass = jnp.where(slots < count, mass_ref[...], 0.0)
    counts = jnp.full((1, 256), count, jnp.int32).astype(F32)
    src = jnp.concatenate([pos_pred, vel_pred, mass, counts], axis=0)
    for k in range(src_ref.shape[0]):
        src_ref[k] = src
    rest = jnp.concatenate([acc, jerk, h, h], axis=0)
    own = pick(jnp.concatenate([src, rest], axis=0), slot_ref[...])
    own_ref[...] = own
    for k in range(act_ref.shape[0]):
        act_ref[k] = own[0:8]


def correct_kernel(own_ref, part_ref, state_ref, deriv_ref, pot_ref):
    summed = part_ref[0]
    for k in range(1, part_ref.shape[0]):
        summed = summed + part_ref[k]
    own = own_ref[...]
    pos_now, vel_now = own[0:3], own[3:6]
    acc_start, jerk_start, step = own[8:11], own[11:14], own[14:15]
    acc_end, jerk_end = summed[0:3], summed[3:6]
    differ = acc_start - acc_end
    fourth = -6.0 * differ - step * (4.0 * jerk_start + 2.0 * jerk_end)
    fifth = 12.0 * differ + 6.0 * step * (jerk_start + jerk_end)
    new_pos = pos_now + step * step / 24.0 * fourth + step * step / 120.0 * fifth
    new_vel = vel_now + step / 6.0 * fourth + step / 24.0 * fifth
    state_ref[...] = jnp.concatenate([new_pos, new_vel], axis=0)
    deriv_ref[...] = summed[0:6]
    pot_ref[...] = summed[6:7]


VM = pl.BlockSpec(memory_space=pltpu.VMEM)
SM = pl.BlockSpec(memory_space=pltpu.SMEM)
SRC_AXES = ("y", "z")
ACT_AXES = ("x", "c")


def shards(positions, velocities, accel_old, jerk_old, masses, levels, live_count, active_slot):
    n_src, n_act = 32, 8
    src, own, act = pl.pallas_call(
        predict_kernel,
        out_shape=(
            jax.ShapeDtypeStruct((n_src, 8, 256), F32),
            jax.ShapeDtypeStruct((16, 128), F32),
            jax.ShapeDtypeStruct((n_act, 8, 128), F32),
        ),
        in_specs=[VM, VM, VM, VM, VM, VM, SM, VM],
        out_specs=(VM, VM, VM),
        name="predict",
    )(positions, velocities, accel_old, jerk_old, masses[None], levels[None], live_count, active_slot[None])
    actives = lax.all_to_all(act, ACT_AXES, 0, 0)
    sources = lax.all_to_all(src, SRC_AXES, 0, 0)
    partial_sums = pair_sums(actives, sources)
    parts = lax.all_to_all(partial_sums, ACT_AXES, 0, 0)
    state, deriv, pot = pl.pallas_call(
        correct_kernel,
        out_shape=(
            jax.ShapeDtypeStruct((6, 128), F32),
            jax.ShapeDtypeStruct((6, 128), F32),
            jax.ShapeDtypeStruct((1, 128), F32),
        ),
        in_specs=[VM, VM],
        out_specs=(VM, VM, VM),
        name="correct",
    )(own, parts)
    return state, deriv, pot[0]


def solution(mesh):
    fine = Mesh(mesh.devices.reshape(4, 4, 8, 2), ("x", "y", "z", "c"))
    every = ("x", "y", "z", "c")
    rows, flat = P(None, every), P(every)
    return jax.shard_map(
        shards,
        mesh=fine,
        in_specs=(rows, rows, rows, rows, flat, flat, flat, flat),
        out_specs=(rows, rows, flat),
        check_vma=False,
    )
```

```python
import functools
import jax
import jax.numpy as jnp
from jax import lax
from jax.experimental import pallas as pl
from jax.experimental.pallas import tpu as pltpu
from jax.sharding import Mesh, PartitionSpec as P

soften_sq = 0.0001
BF = jnp.bfloat16
F32 = jnp.float32


def round_bf(x):
    return x.astype(BF).astype(F32)


def pieces3(x):
    a = round_bf(x)
    r = x - a
    b = round_bf(r)
    return a, b, r - b


def row_ids(shape):
    return lax.broadcasted_iota(jnp.int32, shape, 0)


def grid_split(x):
    row = row_ids(x.shape)
    up = jnp.where(row < 3, 64.0, jnp.where(row < 6, 32.0, 0.0))
    down = jnp.where(row < 3, 1.0 / 64.0, 1.0 / 32.0)
    coarse = jnp.round(x * up) * down
    rest = jnp.where(row < 6, x - coarse, 0.0)
    p1 = round_bf(rest)
    p2 = round_bf(rest - p1)
    return coarse, p1, p2


def twice(t):
    return jnp.where(row_ids(t.shape) < 3, t, pltpu.roll(t, 3, 0))


def squares(coarse, p1, p2):
    fine = p1 + p2
    t, l = twice(coarse), twice(fine)
    return coarse * t, coarse * l + fine * (t + l)


def source_features(x):
    c, p1, p2 = grid_split(x)
    exact, rest = squares(c, p1, p2)
    e1 = round_bf(exact)
    r1, r2, r3 = pieces3(rest)
    one = jnp.ones_like(c)
    zero = jnp.zeros_like(c)
    parts = [e1, exact - e1, one, c, p1, p2, c, c, p1, p2, p1, r1, r2, r3, one, zero]
    return jnp.concatenate([jnp.concatenate(parts[k:k + 2], axis=0).astype(BF) for k in range(0, 16, 2)], axis=0).T


def active_features(x):
    c, p1, p2 = grid_split(x)
    exact, rest = squares(c, p1, p2)
    row = row_ids(x.shape)
    one = jnp.ones_like(c)

    def sums(t, first):
        return jnp.sum(t[first:first + 3], axis=0, keepdims=True)

    def stack(t):
        return jnp.concatenate([*pieces3(t), jnp.zeros((5, t.shape[1]), F32)], axis=0)

    def norm_side(t):
        return jnp.where(row < 3, -2.0 * t, 0.0)

    def dot_side(t):
        return jnp.concatenate([-t[3:6], -t[0:3], jnp.zeros_like(t[6:8])], axis=0)

    def build(side, first, soften):
        pick_rows = jnp.where((row >= first) & (row < first + 3), one, 0.0)
        h, a, b = side(c), side(p1), side(p2)
        same = [pick_rows] * 3
        parts = [*same[:2], stack(sums(exact, first)), h, h, h, a, b, a, a, b, *same, stack(sums(rest, first) + soften), 0.0 * one]
        return jnp.concatenate(parts, axis=0)

    return build(norm_side, 0, soften_sq), build(dot_side, 3, 0.0)


def reduce_rows(x):
    row = row_ids(x.shape)
    c, p1, p2 = grid_split(x)
    near = c + (p1 + p2)
    square = near * near
    norm = square + (pltpu.roll(square, 7, 0) + pltpu.roll(square, 6, 0))
    y = jnp.where(row < 6, near, jnp.where(row == 6, 1.0, pltpu.roll(norm, 7, 0))) * x[6:7]
    a, b, c = pieces3(y)
    return jnp.concatenate([a, b, c, jnp.zeros_like(a)], axis=0)


def split_hi_lo(t):
    hi = t.astype(BF)
    return hi, (t - hi.astype(F32)).astype(BF)


def pair_kernel(n_src, n_act, near_ref, far_ref, src_ref, out_ref, dense, feat_j, feat_q, feat_d, red_ref, acc_u, acc_p, *bufs):
    tile = 256
    n_tiles = n_act * 128 // tile
    me = 2 * lax.axis_index("x") + lax.axis_index("c")

    def active(k):
        return near_ref[k] if k < n_act // 2 else far_ref[k - n_act // 2]

    q_bufs, d_bufs, v_bufs = (bufs[k * n_tiles:(k + 1) * n_tiles] for k in range(3))
    width = n_src * 256 + 768
    for t in range(width // 128):
        dense[:, t * 128:(t + 1) * 128] = jnp.zeros((8, 128), F32)
    lane = lax.broadcasted_iota(jnp.int32, (8, 128), 1)
    counts = [jnp.max(src_ref[b, 7:8, 0:128]).astype(jnp.int32) for b in range(n_src)]
    offset = jnp.int32(0)
    for b in range(n_src):
        shift = lax.rem(offset, 128)
        start = pl.multiple_of(offset - shift, 128)
        left = pltpu.roll(src_ref[b, :, 0:128], shift, 1)
        right = pltpu.roll(src_ref[b, :, 128:256], shift, 1)
        before = lane < shift
        dense[:, pl.ds(start, 128)] = jnp.where(before, dense[:, pl.ds(start, 128)], left)
        dense[:, pl.ds(start + 128, 128)] = jnp.where(before, left, right)
        dense[:, pl.ds(start + 256, 128)] = jnp.where(before, right, 0.0)
        offset = offset + counts[b]
    n_blocks = (offset + (tile - 1)) // tile
    for k in range(n_act):
        fq, fd = active_features(active(k))
        feat_q[k] = fq.astype(BF)
        feat_d[k] = fd.astype(BF)
    acc_u[...] = jnp.zeros_like(acc_u)
    acc_p[...] = jnp.zeros_like(acc_p)

    def sources(b):
        return dense[:, pl.ds(pl.multiple_of(b * tile, tile), tile)]

    def wide(ref, *at):
        return jnp.concatenate([ref[(*at, 0)], ref[(*at, 1)]], axis=1)

    def generate(i):
        fj = feat_j[...]
        fq = jnp.concatenate([feat_q[2 * i], feat_q[2 * i + 1]], axis=1)
        fd = jnp.concatenate([feat_d[2 * i], feat_d[2 * i + 1]], axis=1)
        q_bufs[i][...] = jnp.dot(fj, fq, preferred_element_type=F32)
        d_bufs[i][...] = jnp.dot(fj, fd, preferred_element_type=F32)

    def combine(i):
        v = v_bufs[i]
        for half in range(2):
            lanes = slice(half * 128, half * 128 + 128)
            q = q_bufs[i][:, lanes]
            d = d_bufs[i][:, lanes]
            s = lax.rsqrt(q)
            s2 = s * s
            u = s * s2
            p = (u * s2) * d
            v[0, half], v[1, half] = split_hi_lo(u)
            v[2, half], v[3, half] = split_hi_lo(p)

    def reduce(i):
        v = v_bufs[i]
        lanes = slice(i * tile, (i + 1) * tile)
        rows = red_ref[...]
        two = rows[0:16]

        def mm(a, k):
            return jnp.dot(a, wide(v, k), preferred_element_type=F32)

        ru, rul, rp, rpl = mm(rows, 0), mm(two, 1), mm(rows, 2), mm(two, 3)
        acc_u[:, lanes] += (ru[0:8] + ru[8:16]) + (ru[16:24] + (rul[0:8] + rul[8:16]))
        acc_p[:, lanes] += (rp[0:8] + rp[8:16]) + (rp[16:24] + (rpl[0:8] + rpl[8:16]))

    feat_j[...] = source_features(sources(0))
    for i in range(n_tiles):
        generate(i)
    feat_j[...] = source_features(sources(1))
    red_ref[...] = reduce_rows(sources(0)).astype(BF)
    for i in range(n_tiles):
        combine(i)
        generate(i)
    feat_j[...] = source_features(sources(2))

    def pair(k, _):
        for b in (2 * k + 1, 2 * k + 2):
            fresh = source_features(sources(b + 2))
            rows = reduce_rows(sources(b)).astype(BF)
            for i in range(n_tiles):
                reduce(i)
                combine(i)
                generate(i)
            feat_j[...] = fresh
            red_ref[...] = rows
        return 0

    lax.fori_loop(0, n_blocks // 2, pair, 0)
    for i in range(n_tiles):
        reduce(i)
    for k in range(n_act):
        lanes = slice(k * 128, (k + 1) * 128)
        su = acc_u[:, lanes]
        sp = acc_p[:, lanes]
        st = active(k)
        near = sum(grid_split(st))
        at = near[0:3]
        accel = su[0:3] - at * su[6:7]
        jerk = su[3:6] - near[3:6] * su[6:7] - 3.0 * (sp[0:3] - at * sp[6:7])
        norm = jnp.sum(at * at, axis=0, keepdims=True) + soften_sq
        pot = 2.0 * jnp.sum(at * su[0:3], axis=0, keepdims=True) - su[7:8] - norm * su[6:7]
        out_ref[me ^ PARTNER[k]] = jnp.concatenate([accel, jerk, pot, jnp.zeros((1, 128), F32)], axis=0)


PARTNER = (0, 1, 2, 3, 6, 7, 4, 5)


def pair_sums(near, far, sources):
    n_act, n_src = 2 * near.shape[0], sources.shape[0]
    total = n_act * 128
    return pl.pallas_call(
        functools.partial(pair_kernel, n_src, n_act),
        out_shape=jax.ShapeDtypeStruct((n_act, 8, 128), F32),
        in_specs=[pl.BlockSpec(memory_space=pltpu.VMEM)] * 3,
        out_specs=pl.BlockSpec(memory_space=pltpu.VMEM),
        scratch_shapes=[
            pltpu.VMEM((8, n_src * 256 + 768), F32),
            pltpu.VMEM((256, 128), BF),
            pltpu.VMEM((n_act, 128, 128), BF),
            pltpu.VMEM((n_act, 128, 128), BF),
            pltpu.VMEM((32, 256), BF),
            pltpu.VMEM((8, total), F32),
            pltpu.VMEM((8, total), F32),
            *[pltpu.VMEM((256, 256), F32) for _ in range(2 * (total // 256))],
            *[pltpu.VMEM((4, 2, 256, 128), BF) for _ in range(total // 256)],
        ],
        name="pair_sums",
        cost_estimate=pl.CostEstimate(flops=400_000_000, bytes_accessed=400_000, transcendentals=8_000_000),
    )(near, far, sources)


def pick(table, slot):
    rows = []
    for k in range(table.shape[0] // 8):
        part = table[8 * k:8 * k + 8]
        low = jnp.broadcast_to(lax.rem(slot, 128), (8, 128))
        left = jnp.take_along_axis(part[:, 0:128], low, axis=1)
        right = jnp.take_along_axis(part[:, 128:256], low, axis=1)
        rows.append(jnp.where(slot < 128, left, right))
    return jnp.concatenate(rows, axis=0)


def predict_kernel(pos_ref, vel_ref, acc_ref, jerk_ref, mass_ref, level_ref, live_ref, slot_ref, src_ref, own_ref, act_ref):
    level = level_ref[...]
    half = jnp.where((level & 1) == 1, 0.5, 1.0)
    h = 0.5 * half * jnp.where((level & 2) == 2, 0.25, 1.0)
    acc, jerk, vel = acc_ref[...], jerk_ref[...], vel_ref[...]
    pos_pred = pos_ref[...] + h * (vel + h * (acc / 2.0 + h * jerk / 6.0))
    vel_pred = vel + h * (acc + h * jerk / 2.0)
    slots = lax.broadcasted_iota(jnp.int32, (1, 256), 1)
    count = live_ref[0]
    mass = jnp.where(slots < count, mass_ref[...], 0.0)
    counts = jnp.full((1, 256), count, jnp.int32).astype(F32)
    src = jnp.concatenate([pos_pred, vel_pred, mass, counts], axis=0)
    for k in range(src_ref.shape[0]):
        src_ref[k] = src
    rest = jnp.concatenate([acc, jerk, h, h], axis=0)
    own = pick(jnp.concatenate([src, rest], axis=0), slot_ref[...])
    own_ref[...] = own
    act_ref[0] = own[0:8]


def correct_kernel(own_ref, part_ref, state_ref, deriv_ref, pot_ref):
    summed = part_ref[0]
    for k in range(1, part_ref.shape[0]):
        summed = summed + part_ref[k]
    own = own_ref[...]
    pos_now, vel_now = own[0:3], own[3:6]
    acc_start, jerk_start, step = own[8:11], own[11:14], own[14:15]
    acc_end, jerk_end = summed[0:3], summed[3:6]
    differ = acc_start - acc_end
    fourth = -6.0 * differ - step * (4.0 * jerk_start + 2.0 * jerk_end)
    fifth = 12.0 * differ + 6.0 * step * (jerk_start + jerk_end)
    new_pos = pos_now + step * step / 24.0 * fourth + step * step / 120.0 * fifth
    new_vel = vel_now + step / 6.0 * fourth + step / 24.0 * fifth
    state_ref[...] = jnp.concatenate([new_pos, new_vel], axis=0)
    deriv_ref[...] = summed[0:6]
    pot_ref[...] = summed[6:7]


VM = pl.BlockSpec(memory_space=pltpu.VMEM)
SM = pl.BlockSpec(memory_space=pltpu.SMEM)
SRC_AXES = ("y", "z")
ACT_AXES = ("x", "c")


def shards(positions, velocities, accel_old, jerk_old, masses, levels, live_count, active_slot):
    n_src = 32
    src, own, act = pl.pallas_call(
        predict_kernel,
        out_shape=(
            jax.ShapeDtypeStruct((n_src, 8, 256), F32),
            jax.ShapeDtypeStruct((16, 128), F32),
            jax.ShapeDtypeStruct((1, 8, 128), F32),
        ),
        in_specs=[VM, VM, VM, VM, VM, VM, SM, VM],
        out_specs=(VM, VM, VM),
        name="predict",
    )(positions, velocities, accel_old, jerk_old, masses[None], levels[None], live_count, active_slot[None])
    sources = lax.all_to_all(src, SRC_AXES, 0, 0)
    two = jnp.concatenate([act, lax.ppermute(act, "c", ((0, 1), (1, 0)))])
    four = jnp.concatenate([two, lax.ppermute(two, "x", ((0, 1), (1, 0), (2, 3), (3, 2)))])
    far = lax.ppermute(four, "x", ((0, 3), (3, 0), (1, 2), (2, 1)))
    partial_sums = pair_sums(four, far, sources)
    parts = lax.all_to_all(partial_sums, ACT_AXES, 0, 0)
    state, deriv, pot = pl.pallas_call(
        correct_kernel,
        out_shape=(
            jax.ShapeDtypeStruct((6, 128), F32),
            jax.ShapeDtypeStruct((6, 128), F32),
            jax.ShapeDtypeStruct((1, 128), F32),
        ),
        in_specs=[VM, VM],
        out_specs=(VM, VM, VM),
        name="correct",
    )(own, parts)
    return state, deriv, pot[0]


def solution(mesh):
    fine = Mesh(mesh.devices.reshape(4, 4, 8, 2), ("x", "y", "z", "c"))
    every = ("x", "y", "z", "c")
    rows, flat = P(None, every), P(every)
    return jax.shard_map(
        shards,
        mesh=fine,
        in_specs=(rows, rows, rows, rows, flat, flat, flat, flat),
        out_specs=(rows, rows, flat),
        check_vma=False,
    )
```

```python
import functools
import jax
import jax.numpy as jnp
from jax import lax
from jax.experimental import pallas as pl
from jax.experimental.pallas import tpu as pltpu
from jax.sharding import Mesh, PartitionSpec as P

soften_sq = 0.0001
BF = jnp.bfloat16
F32 = jnp.float32


def in_vmem(x):
    return pltpu.with_memory_space_constraint(x, pltpu.VMEM)


def round_bf(x):
    return x.astype(BF).astype(F32)


def pieces3(x):
    a = round_bf(x)
    r = x - a
    b = round_bf(r)
    return a, b, r - b


def row_ids(shape):
    return lax.broadcasted_iota(jnp.int32, shape, 0)


def grid_split(x):
    row = row_ids(x.shape)
    up = jnp.where(row < 3, 64.0, jnp.where(row < 6, 32.0, 0.0))
    down = jnp.where(row < 3, 1.0 / 64.0, 1.0 / 32.0)
    coarse = jnp.round(x * up) * down
    rest = jnp.where(row < 6, x - coarse, 0.0)
    p1 = round_bf(rest)
    p2 = round_bf(rest - p1)
    return coarse, p1, p2


def twice(t):
    return jnp.where(row_ids(t.shape) < 3, t, pltpu.roll(t, 3, 0))


def squares(coarse, p1, p2):
    fine = p1 + p2
    t, l = twice(coarse), twice(fine)
    return coarse * t, coarse * l + fine * (t + l)


def source_features(x):
    c, p1, p2 = grid_split(x)
    exact, rest = squares(c, p1, p2)
    e1 = round_bf(exact)
    r1, r2, r3 = pieces3(rest)
    one = jnp.ones_like(c)
    zero = jnp.zeros_like(c)
    parts = [e1, exact - e1, one, c, p1, p2, c, c, p1, p2, p1, r1, r2, r3, one, zero]
    return jnp.concatenate([jnp.concatenate(parts[k:k + 2], axis=0).astype(BF) for k in range(0, 16, 2)], axis=0).T


def active_features(x):
    c, p1, p2 = grid_split(x)
    exact, rest = squares(c, p1, p2)
    row = row_ids(x.shape)
    one = jnp.ones_like(c)

    def sums(t, first):
        return jnp.sum(t[first:first + 3], axis=0, keepdims=True)

    def stack(t):
        return jnp.concatenate([*pieces3(t), jnp.zeros((5, t.shape[1]), F32)], axis=0)

    def norm_side(t):
        return jnp.where(row < 3, -2.0 * t, 0.0)

    def dot_side(t):
        return jnp.concatenate([-t[3:6], -t[0:3], jnp.zeros_like(t[6:8])], axis=0)

    def build(side, first, soften):
        pick_rows = jnp.where((row >= first) & (row < first + 3), one, 0.0)
        h, a, b = side(c), side(p1), side(p2)
        same = [pick_rows] * 3
        parts = [*same[:2], stack(sums(exact, first)), h, h, h, a, b, a, a, b, *same, stack(sums(rest, first) + soften), 0.0 * one]
        return jnp.concatenate(parts, axis=0)

    return build(norm_side, 0, soften_sq), build(dot_side, 3, 0.0)


def reduce_rows(x):
    row = row_ids(x.shape)
    c, p1, p2 = grid_split(x)
    near = c + (p1 + p2)
    square = near * near
    norm = square + (pltpu.roll(square, 7, 0) + pltpu.roll(square, 6, 0))
    y = jnp.where(row < 6, near, jnp.where(row == 6, 1.0, pltpu.roll(norm, 7, 0))) * x[6:7]
    a, b, c = pieces3(y)
    return jnp.concatenate([a, b, c, jnp.zeros_like(a)], axis=0)


def split_hi_lo(t):
    hi = t.astype(BF)
    return hi, (t - hi.astype(F32)).astype(BF)


def pair_kernel(n_src, n_act, near_ref, far_ref, src_ref, out_ref, dense, feat_j, feat_q, feat_d, red_ref, acc_u, acc_p, *bufs):
    tile = 256
    n_tiles = n_act * 128 // tile
    me = 2 * lax.axis_index("x") + lax.axis_index("c")

    def active(k):
        return near_ref[k] if k < n_act // 2 else far_ref[k - n_act // 2]

    q_bufs, d_bufs, v_bufs = (bufs[k * n_tiles:(k + 1) * n_tiles] for k in range(3))
    dense[...] = jnp.zeros_like(dense)
    lane = lax.broadcasted_iota(jnp.int32, (8, 128), 1)
    counts = [jnp.max(src_ref[b, 7:8, 0:128]).astype(jnp.int32) for b in range(n_src)]
    offset = jnp.int32(0)
    for b in range(n_src):
        shift = offset & 127
        at = offset >> 7
        left = pltpu.roll(src_ref[b, :, 0:128], shift, 1)
        right = pltpu.roll(src_ref[b, :, 128:256], shift, 1)
        before = lane < shift
        dense[at] = jnp.where(before, dense[at], left)
        dense[at + 1] = jnp.where(before, left, right)
        dense[at + 2] = jnp.where(before, right, 0.0)
        offset = offset + counts[b]
    n_blocks = (offset + (tile - 1)) >> 8
    for k in range(n_act):
        fq, fd = active_features(active(k))
        feat_q[k] = fq.astype(BF)
        feat_d[k] = fd.astype(BF)
    acc_u[...] = jnp.zeros_like(acc_u)
    acc_p[...] = jnp.zeros_like(acc_p)

    def sources(b):
        return jnp.concatenate([dense[2 * b], dense[2 * b + 1]], axis=1)

    def wide(ref, *at):
        return jnp.concatenate([ref[(*at, 0)], ref[(*at, 1)]], axis=1)

    def generate(i):
        fj = feat_j[...]
        fq = jnp.concatenate([feat_q[2 * i], feat_q[2 * i + 1]], axis=1)
        fd = jnp.concatenate([feat_d[2 * i], feat_d[2 * i + 1]], axis=1)
        q_bufs[i][...] = jnp.dot(fj, fq, preferred_element_type=F32)
        d_bufs[i][...] = jnp.dot(fj, fd, preferred_element_type=F32)

    def combine(i):
        v = v_bufs[i]
        for half in range(2):
            lanes = slice(half * 128, half * 128 + 128)
            q = q_bufs[i][:, lanes]
            d = d_bufs[i][:, lanes]
            s = lax.rsqrt(q)
            s2 = s * s
            u = s * s2
            p = (u * s2) * d
            v[0, half], v[1, half] = split_hi_lo(u)
            v[2, half], v[3, half] = split_hi_lo(p)

    def reduce(i):
        v = v_bufs[i]
        lanes = slice(i * tile, (i + 1) * tile)
        rows = red_ref[...]
        two = rows[0:16]

        def mm(a, k):
            return jnp.dot(a, wide(v, k), preferred_element_type=F32)

        ru, rul, rp, rpl = mm(rows, 0), mm(two, 1), mm(rows, 2), mm(two, 3)
        acc_u[:, lanes] += (ru[0:8] + ru[8:16]) + (ru[16:24] + (rul[0:8] + rul[8:16]))
        acc_p[:, lanes] += (rp[0:8] + rp[8:16]) + (rp[16:24] + (rpl[0:8] + rpl[8:16]))

    feat_j[...] = source_features(sources(0))
    for i in range(n_tiles):
        generate(i)
    feat_j[...] = source_features(sources(1))
    red_ref[...] = reduce_rows(sources(0)).astype(BF)
    for i in range(n_tiles):
        combine(i)
        generate(i)
    feat_j[...] = source_features(sources(2))

    def pair(k, _):
        for b in (2 * k + 1, 2 * k + 2):
            fresh = source_features(sources(b + 2))
            rows = reduce_rows(sources(b)).astype(BF)
            for i in range(n_tiles):
                reduce(i)
                combine(i)
                generate(i)
            feat_j[...] = fresh
            red_ref[...] = rows
        return 0

    lax.fori_loop(0, n_blocks // 2, pair, 0)
    for i in range(n_tiles):
        reduce(i)
    for k in range(n_act):
        lanes = slice(k * 128, (k + 1) * 128)
        su = acc_u[:, lanes]
        sp = acc_p[:, lanes]
        st = active(k)
        near = sum(grid_split(st))
        at = near[0:3]
        accel = su[0:3] - at * su[6:7]
        jerk = su[3:6] - near[3:6] * su[6:7] - 3.0 * (sp[0:3] - at * sp[6:7])
        norm = jnp.sum(at * at, axis=0, keepdims=True) + soften_sq
        pot = 2.0 * jnp.sum(at * su[0:3], axis=0, keepdims=True) - su[7:8] - norm * su[6:7]
        out_ref[me ^ PARTNER[k]] = jnp.concatenate([accel, jerk, pot, jnp.zeros((1, 128), F32)], axis=0)


PARTNER = (0, 1, 2, 3, 6, 7, 4, 5)


def pair_sums(near, far, sources):
    n_act, n_src = 2 * near.shape[0], sources.shape[0]
    total = n_act * 128
    return pl.pallas_call(
        functools.partial(pair_kernel, n_src, n_act),
        out_shape=pltpu.VMEM((n_act, 8, 128), F32),
        in_specs=[pl.BlockSpec(memory_space=pltpu.VMEM)] * 3,
        out_specs=pl.BlockSpec(memory_space=pltpu.VMEM),
        scratch_shapes=[
            pltpu.VMEM((2 * n_src + 6, 8, 128), F32),
            pltpu.VMEM((256, 128), BF),
            pltpu.VMEM((n_act, 128, 128), BF),
            pltpu.VMEM((n_act, 128, 128), BF),
            pltpu.VMEM((32, 256), BF),
            pltpu.VMEM((8, total), F32),
            pltpu.VMEM((8, total), F32),
            *[pltpu.VMEM((256, 256), F32) for _ in range(2 * (total // 256))],
            *[pltpu.VMEM((4, 2, 256, 128), BF) for _ in range(total // 256)],
        ],
        name="pair_sums",
        cost_estimate=pl.CostEstimate(flops=400_000_000, bytes_accessed=400_000, transcendentals=8_000_000),
    )(*map(in_vmem, (near, far, sources)))


def pick(table, slot):
    rows = []
    for k in range(table.shape[0] // 8):
        part = table[8 * k:8 * k + 8]
        low = jnp.broadcast_to(lax.rem(slot, 128), (8, 128))
        left = jnp.take_along_axis(part[:, 0:128], low, axis=1)
        right = jnp.take_along_axis(part[:, 128:256], low, axis=1)
        rows.append(jnp.where(slot < 128, left, right))
    return jnp.concatenate(rows, axis=0)


def predict_kernel(pos_ref, vel_ref, acc_ref, jerk_ref, mass_ref, level_ref, live_ref, slot_ref, src_ref, own_ref, act_ref):
    level = level_ref[...]
    half = jnp.where((level & 1) == 1, 0.5, 1.0)
    h = 0.5 * half * jnp.where((level & 2) == 2, 0.25, 1.0)
    acc, jerk, vel = acc_ref[...], jerk_ref[...], vel_ref[...]
    pos_pred = pos_ref[...] + h * (vel + h * (acc / 2.0 + h * jerk / 6.0))
    vel_pred = vel + h * (acc + h * jerk / 2.0)
    slots = lax.broadcasted_iota(jnp.int32, (1, 256), 1)
    count = live_ref[0]
    mass = jnp.where(slots < count, mass_ref[...], 0.0)
    counts = jnp.full((1, 256), count, jnp.int32).astype(F32)
    src = jnp.concatenate([pos_pred, vel_pred, mass, counts], axis=0)
    for k in range(src_ref.shape[0]):
        src_ref[k] = src
    rest = jnp.concatenate([acc, jerk, h, h], axis=0)
    own = pick(jnp.concatenate([src, rest], axis=0), slot_ref[...])
    own_ref[...] = own
    act_ref[0] = own[0:8]


def correct_kernel(own_ref, part_ref, state_ref, deriv_ref, pot_ref):
    summed = part_ref[0]
    for k in range(1, part_ref.shape[0]):
        summed = summed + part_ref[k]
    own = own_ref[...]
    pos_now, vel_now = own[0:3], own[3:6]
    acc_start, jerk_start, step = own[8:11], own[11:14], own[14:15]
    acc_end, jerk_end = summed[0:3], summed[3:6]
    differ = acc_start - acc_end
    fourth = -6.0 * differ - step * (4.0 * jerk_start + 2.0 * jerk_end)
    fifth = 12.0 * differ + 6.0 * step * (jerk_start + jerk_end)
    new_pos = pos_now + step * step / 24.0 * fourth + step * step / 120.0 * fifth
    new_vel = vel_now + step / 6.0 * fourth + step / 24.0 * fifth
    state_ref[...] = jnp.concatenate([new_pos, new_vel], axis=0)
    deriv_ref[...] = summed[0:6]
    pot_ref[...] = summed[6:7]


VM = pl.BlockSpec(memory_space=pltpu.VMEM)
SM = pl.BlockSpec(memory_space=pltpu.SMEM)
SRC_AXES = ("y", "z")
ACT_AXES = ("x", "c")


def shards(positions, velocities, accel_old, jerk_old, masses, levels, live_count, active_slot):
    n_src = 32
    src, own, act = pl.pallas_call(
        predict_kernel,
        out_shape=(
            pltpu.VMEM((n_src, 8, 256), F32),
            pltpu.VMEM((16, 128), F32),
            pltpu.VMEM((1, 8, 128), F32),
        ),
        in_specs=[VM, VM, VM, VM, VM, VM, SM, VM],
        out_specs=(VM, VM, VM),
        name="predict",
    )(positions, velocities, accel_old, jerk_old, masses[None], levels[None], live_count, active_slot[None])
    sources = lax.all_to_all(src, SRC_AXES, 0, 0)
    two = jnp.concatenate([act, lax.ppermute(act, "c", ((0, 1), (1, 0)))])
    four = jnp.concatenate([two, lax.ppermute(two, "x", ((0, 1), (1, 0), (2, 3), (3, 2)))])
    far = lax.ppermute(four, "x", ((0, 3), (3, 0), (1, 2), (2, 1)))
    partial_sums = pair_sums(four, far, sources)
    parts = lax.all_to_all(partial_sums, ACT_AXES, 0, 0)
    state, deriv, pot = pl.pallas_call(
        correct_kernel,
        out_shape=(
            jax.ShapeDtypeStruct((6, 128), F32),
            jax.ShapeDtypeStruct((6, 128), F32),
            jax.ShapeDtypeStruct((1, 128), F32),
        ),
        in_specs=[VM, VM],
        out_specs=(VM, VM, VM),
        name="correct",
    )(in_vmem(own), in_vmem(parts))
    return state, deriv, pot[0]


def solution(mesh):
    fine = Mesh(mesh.devices.reshape(4, 4, 8, 2), ("x", "y", "z", "c"))
    every = ("x", "y", "z", "c")
    rows, flat = P(None, every), P(every)
    return jax.shard_map(
        shards,
        mesh=fine,
        in_specs=(rows, rows, rows, rows, flat, flat, flat, flat),
        out_specs=(rows, rows, flat),
        check_vma=False,
    )
```

```python
import functools
import jax
import jax.numpy as jnp
from jax import lax
from jax.experimental import pallas as pl
from jax.experimental.pallas import tpu as pltpu
from jax.sharding import Mesh, PartitionSpec as P

soften_sq = 0.0001
BF = jnp.bfloat16
F32 = jnp.float32


def in_vmem(x):
    return pltpu.with_memory_space_constraint(x, pltpu.VMEM)


def round_bf(x):
    return x.astype(BF).astype(F32)


def pieces3(x):
    a = round_bf(x)
    r = x - a
    b = round_bf(r)
    return a, b, r - b


def row_ids(shape):
    return lax.broadcasted_iota(jnp.int32, shape, 0)


def grid_split(x):
    row = row_ids(x.shape)
    up = jnp.where(row < 3, 64.0, jnp.where(row < 6, 32.0, 0.0))
    down = jnp.where(row < 3, 1.0 / 64.0, 1.0 / 32.0)
    coarse = jnp.round(x * up) * down
    rest = jnp.where(row < 6, x - coarse, 0.0)
    p1 = round_bf(rest)
    p2 = round_bf(rest - p1)
    return coarse, p1, p2


def twice(t):
    return jnp.where(row_ids(t.shape) < 3, t, pltpu.roll(t, 3, 0))


def squares(coarse, p1, p2):
    fine = p1 + p2
    t, l = twice(coarse), twice(fine)
    return coarse * t, coarse * l + fine * (t + l)


def source_features(x):
    c, p1, p2 = grid_split(x)
    exact, rest = squares(c, p1, p2)
    e1 = round_bf(exact)
    r1, r2, r3 = pieces3(rest)
    one = jnp.ones_like(c)
    zero = jnp.zeros_like(c)
    parts = [e1, exact - e1, one, c, p1, p2, c, c, p1, p2, p1, r1, r2, r3, one, zero]
    return jnp.concatenate([jnp.concatenate(parts[k:k + 2], axis=0).astype(BF) for k in range(0, 16, 2)], axis=0).T


def active_features(x):
    c, p1, p2 = grid_split(x)
    exact, rest = squares(c, p1, p2)
    row = row_ids(x.shape)
    one = jnp.ones_like(c)

    def sums(t, first):
        return jnp.sum(t[first:first + 3], axis=0, keepdims=True)

    def stack(t):
        return jnp.concatenate([*pieces3(t), jnp.zeros((5, t.shape[1]), F32)], axis=0)

    def norm_side(t):
        return jnp.where(row < 3, -2.0 * t, 0.0)

    def dot_side(t):
        return jnp.concatenate([-t[3:6], -t[0:3], jnp.zeros_like(t[6:8])], axis=0)

    def build(side, first, soften):
        pick_rows = jnp.where((row >= first) & (row < first + 3), one, 0.0)
        h, a, b = side(c), side(p1), side(p2)
        same = [pick_rows] * 3
        parts = [*same[:2], stack(sums(exact, first)), h, h, h, a, b, a, a, b, *same, stack(sums(rest, first) + soften), 0.0 * one]
        return jnp.concatenate(parts, axis=0)

    return build(norm_side, 0, soften_sq), build(dot_side, 3, 0.0)


def reduce_rows(x):
    row = row_ids(x.shape)
    c, p1, p2 = grid_split(x)
    near = c + (p1 + p2)
    square = near * near
    norm = square + (pltpu.roll(square, 7, 0) + pltpu.roll(square, 6, 0))
    y = jnp.where(row < 6, near, jnp.where(row == 6, 1.0, pltpu.roll(norm, 7, 0))) * x[6:7]
    a, b, c = pieces3(y)
    return jnp.concatenate([a, b, c, jnp.zeros_like(a)], axis=0)


def split_hi_lo(t):
    hi = t.astype(BF)
    return hi, (t - hi.astype(F32)).astype(BF)


def pair_kernel(n_src, n_act, near_ref, far_ref, src_ref, out_ref, dense, feat_j, feat_q, feat_d, red_ref, acc_u, acc_p, *bufs):
    tile = 256
    n_tiles = n_act * 128 // tile
    me = 2 * lax.axis_index("x") + lax.axis_index("c")

    def active(k):
        return near_ref[k] if k < n_act // 2 else far_ref[k - n_act // 2]

    q_bufs, d_bufs, v_bufs = (bufs[k * n_tiles:(k + 1) * n_tiles] for k in range(3))
    dense[...] = jnp.zeros_like(dense)
    lane = lax.broadcasted_iota(jnp.int32, (8, 128), 1)
    counts = [jnp.max(src_ref[b, 7:8, 0:128]).astype(jnp.int32) for b in range(n_src)]
    offset = jnp.int32(0)
    for b in range(n_src):
        shift = offset & 127
        at = offset >> 7
        left = pltpu.roll(src_ref[b, :, 0:128], shift, 1)
        right = pltpu.roll(src_ref[b, :, 128:256], shift, 1)
        before = lane < shift
        dense[at] = jnp.where(before, dense[at], left)
        dense[at + 1] = jnp.where(before, left, right)
        dense[at + 2] = jnp.where(before, right, 0.0)
        offset = offset + counts[b]
    n_blocks = (offset + (tile - 1)) >> 8
    for k in range(n_act):
        fq, fd = active_features(active(k))
        feat_q[k] = fq.astype(BF)
        feat_d[k] = fd.astype(BF)
    acc_u[...] = jnp.zeros_like(acc_u)
    acc_p[...] = jnp.zeros_like(acc_p)

    def sources(b):
        return jnp.concatenate([dense[2 * b], dense[2 * b + 1]], axis=1)

    def wide(ref, *at):
        return jnp.concatenate([ref[(*at, 0)], ref[(*at, 1)]], axis=1)

    def generate(i):
        fj = feat_j[...]
        fq = jnp.concatenate([feat_q[2 * i], feat_q[2 * i + 1]], axis=1)
        fd = jnp.concatenate([feat_d[2 * i], feat_d[2 * i + 1]], axis=1)
        q_bufs[i][...] = jnp.dot(fj, fq, preferred_element_type=F32)
        d_bufs[i][...] = jnp.dot(fj, fd, preferred_element_type=F32)

    def combine(i):
        v = v_bufs[i]
        for half in range(2):
            lanes = slice(half * 128, half * 128 + 128)
            q = q_bufs[i][:, lanes]
            d = d_bufs[i][:, lanes]
            s = lax.rsqrt(q)
            s2 = s * s
            u = s * s2
            p = (u * s2) * d
            v[0, half], v[1, half] = split_hi_lo(u)
            v[2, half], v[3, half] = split_hi_lo(p)

    def reduce(i):
        v = v_bufs[i]
        lanes = slice(i * tile, (i + 1) * tile)
        rows = red_ref[...]
        two = rows[0:16]

        def mm(a, k):
            return jnp.dot(a, wide(v, k), preferred_element_type=F32)

        ru, rul, rp, rpl = mm(rows, 0), mm(two, 1), mm(rows, 2), mm(two, 3)
        acc_u[:, lanes] += (ru[0:8] + ru[8:16]) + (ru[16:24] + (rul[0:8] + rul[8:16]))
        acc_p[:, lanes] += (rp[0:8] + rp[8:16]) + (rp[16:24] + (rpl[0:8] + rpl[8:16]))

    feat_j[...] = source_features(sources(0))
    for i in range(n_tiles):
        generate(i)
    feat_j[...] = source_features(sources(1))
    red_ref[...] = reduce_rows(sources(0)).astype(BF)
    for i in range(n_tiles):
        combine(i)
        generate(i)
    feat_j[...] = source_features(sources(2))

    def several(first, count):
        def body(k, _):
            for j in range(count):
                b = first + count * k + j
                fresh = source_features(sources(b + 2))
                rows = reduce_rows(sources(b)).astype(BF)
                for i in range(n_tiles):
                    reduce(i)
                    combine(i)
                    generate(i)
                feat_j[...] = fresh
                red_ref[...] = rows
            return 0

        return body

    rest = n_blocks - 1
    lax.fori_loop(0, rest >> 2, several(1, 4), 0)
    lax.fori_loop(0, (rest >> 1) & 1, several(1 + (rest & -4), 2), 0)
    lax.fori_loop(0, rest & 1, several(1 + (rest & -2), 1), 0)
    for i in range(n_tiles):
        reduce(i)
    for k in range(n_act):
        lanes = slice(k * 128, (k + 1) * 128)
        su = acc_u[:, lanes]
        sp = acc_p[:, lanes]
        st = active(k)
        near = sum(grid_split(st))
        at = near[0:3]
        accel = su[0:3] - at * su[6:7]
        jerk = su[3:6] - near[3:6] * su[6:7] - 3.0 * (sp[0:3] - at * sp[6:7])
        norm = jnp.sum(at * at, axis=0, keepdims=True) + soften_sq
        pot = 2.0 * jnp.sum(at * su[0:3], axis=0, keepdims=True) - su[7:8] - norm * su[6:7]
        out_ref[me ^ PARTNER[k]] = jnp.concatenate([accel, jerk, pot, jnp.zeros((1, 128), F32)], axis=0)


PARTNER = (0, 1, 2, 3, 6, 7, 4, 5)


def pair_sums(near, far, sources):
    n_act, n_src = 2 * near.shape[0], sources.shape[0]
    total = n_act * 128
    return pl.pallas_call(
        functools.partial(pair_kernel, n_src, n_act),
        out_shape=pltpu.VMEM((n_act, 8, 128), F32),
        in_specs=[pl.BlockSpec(memory_space=pltpu.VMEM)] * 3,
        out_specs=pl.BlockSpec(memory_space=pltpu.VMEM),
        scratch_shapes=[
            pltpu.VMEM((2 * n_src + 6, 8, 128), F32),
            pltpu.VMEM((256, 128), BF),
            pltpu.VMEM((n_act, 128, 128), BF),
            pltpu.VMEM((n_act, 128, 128), BF),
            pltpu.VMEM((32, 256), BF),
            pltpu.VMEM((8, total), F32),
            pltpu.VMEM((8, total), F32),
            *[pltpu.VMEM((256, 256), F32) for _ in range(2 * (total // 256))],
            *[pltpu.VMEM((4, 2, 256, 128), BF) for _ in range(total // 256)],
        ],
        name="pair_sums",
        cost_estimate=pl.CostEstimate(flops=400_000_000, bytes_accessed=400_000, transcendentals=8_000_000),
    )(*map(in_vmem, (near, far, sources)))


def pick(table, slot):
    rows = []
    for k in range(table.shape[0] // 8):
        part = table[8 * k:8 * k + 8]
        low = jnp.broadcast_to(lax.rem(slot, 128), (8, 128))
        left = jnp.take_along_axis(part[:, 0:128], low, axis=1)
        right = jnp.take_along_axis(part[:, 128:256], low, axis=1)
        rows.append(jnp.where(slot < 128, left, right))
    return jnp.concatenate(rows, axis=0)


def predict_kernel(pos_ref, vel_ref, acc_ref, jerk_ref, mass_ref, level_ref, live_ref, slot_ref, src_ref, own_ref, act_ref):
    level = level_ref[...]
    half = jnp.where((level & 1) == 1, 0.5, 1.0)
    h = 0.5 * half * jnp.where((level & 2) == 2, 0.25, 1.0)
    acc, jerk, vel = acc_ref[...], jerk_ref[...], vel_ref[...]
    pos_pred = pos_ref[...] + h * (vel + h * (acc / 2.0 + h * jerk / 6.0))
    vel_pred = vel + h * (acc + h * jerk / 2.0)
    slots = lax.broadcasted_iota(jnp.int32, (1, 256), 1)
    count = live_ref[0]
    mass = jnp.where(slots < count, mass_ref[...], 0.0)
    counts = jnp.full((1, 256), count, jnp.int32).astype(F32)
    src = jnp.concatenate([pos_pred, vel_pred, mass, counts], axis=0)
    for k in range(src_ref.shape[0]):
        src_ref[k] = src
    rest = jnp.concatenate([acc, jerk, h, h], axis=0)
    own = pick(jnp.concatenate([src, rest], axis=0), slot_ref[...])
    own_ref[...] = own
    act_ref[0] = own[0:8]


def correct_kernel(own_ref, part_ref, state_ref, deriv_ref, pot_ref):
    summed = part_ref[0]
    for k in range(1, part_ref.shape[0]):
        summed = summed + part_ref[k]
    own = own_ref[...]
    pos_now, vel_now = own[0:3], own[3:6]
    acc_start, jerk_start, step = own[8:11], own[11:14], own[14:15]
    acc_end, jerk_end = summed[0:3], summed[3:6]
    differ = acc_start - acc_end
    fourth = -6.0 * differ - step * (4.0 * jerk_start + 2.0 * jerk_end)
    fifth = 12.0 * differ + 6.0 * step * (jerk_start + jerk_end)
    new_pos = pos_now + step * step / 24.0 * fourth + step * step / 120.0 * fifth
    new_vel = vel_now + step / 6.0 * fourth + step / 24.0 * fifth
    state_ref[...] = jnp.concatenate([new_pos, new_vel], axis=0)
    deriv_ref[...] = summed[0:6]
    pot_ref[...] = summed[6:7]


VM = pl.BlockSpec(memory_space=pltpu.VMEM)
SM = pl.BlockSpec(memory_space=pltpu.SMEM)
SRC_AXES = ("y", "z")
ACT_AXES = ("x", "c")


def shards(positions, velocities, accel_old, jerk_old, masses, levels, live_count, active_slot):
    n_src = 32
    src, own, act = pl.pallas_call(
        predict_kernel,
        out_shape=(
            pltpu.VMEM((n_src, 8, 256), F32),
            pltpu.VMEM((16, 128), F32),
            pltpu.VMEM((1, 8, 128), F32),
        ),
        in_specs=[VM, VM, VM, VM, VM, VM, SM, VM],
        out_specs=(VM, VM, VM),
        name="predict",
    )(positions, velocities, accel_old, jerk_old, masses[None], levels[None], live_count, active_slot[None])
    sources = lax.all_to_all(src, SRC_AXES, 0, 0)
    two = jnp.concatenate([act, lax.ppermute(act, "c", ((0, 1), (1, 0)))])
    four = jnp.concatenate([two, lax.ppermute(two, "x", ((0, 1), (1, 0), (2, 3), (3, 2)))])
    far = lax.ppermute(four, "x", ((0, 3), (3, 0), (1, 2), (2, 1)))
    partial_sums = pair_sums(four, far, sources)
    parts = lax.all_to_all(partial_sums, ACT_AXES, 0, 0)
    state, deriv, pot = pl.pallas_call(
        correct_kernel,
        out_shape=(
            jax.ShapeDtypeStruct((6, 128), F32),
            jax.ShapeDtypeStruct((6, 128), F32),
            jax.ShapeDtypeStruct((1, 128), F32),
        ),
        in_specs=[VM, VM],
        out_specs=(VM, VM, VM),
        name="correct",
    )(in_vmem(own), in_vmem(parts))
    return state, deriv, pot[0]


def solution(mesh):
    fine = Mesh(mesh.devices.reshape(4, 4, 8, 2), ("x", "y", "z", "c"))
    every = ("x", "y", "z", "c")
    rows, flat = P(None, every), P(every)
    return jax.shard_map(
        shards,
        mesh=fine,
        in_specs=(rows, rows, rows, rows, flat, flat, flat, flat),
        out_specs=(rows, rows, flat),
        check_vma=False,
    )
```

```python
import functools
import jax
import jax.numpy as jnp
from jax import lax
from jax.experimental import pallas as pl
from jax.experimental.pallas import tpu as pltpu
from jax.sharding import Mesh, PartitionSpec as P

soften_sq = 0.0001
BF = jnp.bfloat16
F32 = jnp.float32


def in_vmem(x):
    return pltpu.with_memory_space_constraint(x, pltpu.VMEM)


def round_bf(x):
    return x.astype(BF).astype(F32)


def pieces3(x):
    a = round_bf(x)
    r = x - a
    b = round_bf(r)
    return a, b, r - b


def row_ids(shape):
    return lax.broadcasted_iota(jnp.int32, shape, 0)


def grid_split(x):
    row = row_ids(x.shape)
    up = jnp.where(row < 3, 64.0, jnp.where(row < 6, 32.0, 0.0))
    down = jnp.where(row < 3, 1.0 / 64.0, 1.0 / 32.0)
    coarse = jnp.round(x * up) * down
    rest = jnp.where(row < 6, x - coarse, 0.0)
    p1 = round_bf(rest)
    p2 = round_bf(rest - p1)
    return coarse, p1, p2


def twice(t):
    return jnp.where(row_ids(t.shape) < 3, t, pltpu.roll(t, 3, 0))


def squares(coarse, p1, p2):
    fine = p1 + p2
    t, l = twice(coarse), twice(fine)
    return coarse * t, coarse * l + fine * (t + l)


def source_features(x):
    c, p1, p2 = grid_split(x)
    exact, rest = squares(c, p1, p2)
    e1 = round_bf(exact)
    r1, r2, r3 = pieces3(rest)
    one = jnp.ones_like(c)
    zero = jnp.zeros_like(c)
    parts = [e1, exact - e1, one, c, p1, p2, c, c, p1, p2, p1, r1, r2, r3, one, zero]
    return jnp.concatenate([jnp.concatenate(parts[k:k + 2], axis=0).astype(BF) for k in range(0, 16, 2)], axis=0).T


def active_features(x):
    c, p1, p2 = grid_split(x)
    exact, rest = squares(c, p1, p2)
    row = row_ids(x.shape)
    one = jnp.ones_like(c)

    def sums(t, first):
        return jnp.sum(t[first:first + 3], axis=0, keepdims=True)

    def stack(t):
        return jnp.concatenate([*pieces3(t), jnp.zeros((5, t.shape[1]), F32)], axis=0)

    def norm_side(t):
        return jnp.where(row < 3, -2.0 * t, 0.0)

    def dot_side(t):
        return jnp.concatenate([-t[3:6], -t[0:3], jnp.zeros_like(t[6:8])], axis=0)

    def build(side, first, soften):
        pick_rows = jnp.where((row >= first) & (row < first + 3), one, 0.0)
        h, a, b = side(c), side(p1), side(p2)
        same = [pick_rows] * 3
        parts = [*same[:2], stack(sums(exact, first)), h, h, h, a, b, a, a, b, *same, stack(sums(rest, first) + soften), 0.0 * one]
        return jnp.concatenate(parts, axis=0)

    return build(norm_side, 0, soften_sq), build(dot_side, 3, 0.0)


def reduce_rows(x):
    row = row_ids(x.shape)
    c, p1, p2 = grid_split(x)
    near = c + (p1 + p2)
    square = near * near
    norm = square + (pltpu.roll(square, 7, 0) + pltpu.roll(square, 6, 0))
    y = jnp.where(row < 6, near, jnp.where(row == 6, 1.0, pltpu.roll(norm, 7, 0))) * x[6:7]
    a, b, c = pieces3(y)
    return jnp.concatenate([a, b, c, jnp.zeros_like(a)], axis=0)


def split_hi_lo(t):
    hi = t.astype(BF)
    return hi, (t - hi.astype(F32)).astype(BF)


def pair_kernel(n_src, n_act, near_ref, far_ref, src_ref, out_ref, dense, feat_j, feat_q, feat_d, red_ref, acc_u, acc_p, *bufs):
    tile = 256
    n_tiles = n_act * 128 // tile
    me = 2 * lax.axis_index("x") + lax.axis_index("c")

    def active(k):
        return near_ref[k] if k < n_act // 2 else far_ref[k - n_act // 2]

    q_bufs, d_bufs, v_bufs = (bufs[k * n_tiles:(k + 1) * n_tiles] for k in range(3))
    dense[...] = jnp.zeros_like(dense)
    lane = lax.broadcasted_iota(jnp.int32, (8, 128), 1)
    counts = [jnp.max(src_ref[b, 7:8, 0:128]).astype(jnp.int32) for b in range(n_src)]
    offset = jnp.int32(0)
    for b in range(n_src):
        shift = offset & 127
        at = offset >> 7
        left = pltpu.roll(src_ref[b, :, 0:128], shift, 1)
        right = pltpu.roll(src_ref[b, :, 128:256], shift, 1)
        before = lane < shift
        dense[at] = jnp.where(before, dense[at], left)
        dense[at + 1] = jnp.where(before, left, right)
        dense[at + 2] = jnp.where(before, right, 0.0)
        offset = offset + counts[b]
    n_blocks = (offset + (tile - 1)) >> 8
    for k in range(n_act):
        fq, fd = active_features(active(k))
        feat_q[k] = fq.astype(BF)
        feat_d[k] = fd.astype(BF)
    acc_u[...] = jnp.zeros_like(acc_u)
    acc_p[...] = jnp.zeros_like(acc_p)

    def sources(b):
        return jnp.concatenate([dense[2 * b], dense[2 * b + 1]], axis=1)

    def wide(ref, *at):
        return jnp.concatenate([ref[(*at, 0)], ref[(*at, 1)]], axis=1)

    def generate(i):
        fj = feat_j[...]
        fq = jnp.concatenate([feat_q[2 * i], feat_q[2 * i + 1]], axis=1)
        fd = jnp.concatenate([feat_d[2 * i], feat_d[2 * i + 1]], axis=1)
        q_bufs[i][...] = jnp.dot(fj, fq, preferred_element_type=F32)
        d_bufs[i][...] = jnp.dot(fj, fd, preferred_element_type=F32)

    def combine(i):
        v = v_bufs[i]
        for half in range(2):
            lanes = slice(half * 128, half * 128 + 128)
            q = q_bufs[i][:, lanes]
            d = d_bufs[i][:, lanes]
            s = lax.rsqrt(q)
            s2 = s * s
            u = s * s2
            p = (u * s2) * d
            v[0, half], v[1, half] = split_hi_lo(u)
            v[2, half], v[3, half] = split_hi_lo(p)

    def reduce(i):
        v = v_bufs[i]
        lanes = slice(i * tile, (i + 1) * tile)
        rows = red_ref[...]
        two = rows[0:16]

        def mm(a, k):
            return jnp.dot(a, wide(v, k), preferred_element_type=F32)

        ru, rul, rp, rpl = mm(rows, 0), mm(two, 1), mm(rows, 2), mm(two, 3)
        acc_u[:, lanes] += (ru[0:8] + ru[8:16]) + (ru[16:24] + (rul[0:8] + rul[8:16]))
        acc_p[:, lanes] += (rp[0:8] + rp[8:16]) + (rp[16:24] + (rpl[0:8] + rpl[8:16]))

    feat_j[...] = source_features(sources(0))
    for i in range(n_tiles):
        generate(i)
    feat_j[...] = source_features(sources(1))
    red_ref[...] = reduce_rows(sources(0)).astype(BF)
    for i in range(n_tiles):
        combine(i)
        generate(i)
    feat_j[...] = source_features(sources(2))

    def several(first, count):
        def body(k, _):
            for j in range(count):
                b = first + count * k + j
                fresh = source_features(sources(b + 2))
                rows = reduce_rows(sources(b)).astype(BF)
                for i in range(n_tiles):
                    reduce(i)
                    combine(i)
                    generate(i)
                feat_j[...] = fresh
                red_ref[...] = rows
            return 0

        return body

    rest = jnp.maximum(n_blocks - 2, 0)
    lax.fori_loop(0, rest >> 2, several(1, 4), 0)
    lax.fori_loop(0, (rest >> 1) & 1, several(1 + (rest & -4), 2), 0)
    lax.fori_loop(0, rest & 1, several(1 + (rest & -2), 1), 0)
    rows = reduce_rows(sources(jnp.maximum(n_blocks - 1, 1))).astype(BF)
    for i in range(n_tiles):
        reduce(i)
        combine(i)
    red_ref[...] = rows
    for i in range(n_tiles):
        reduce(i)
    for k in range(n_act):
        lanes = slice(k * 128, (k + 1) * 128)
        su = acc_u[:, lanes]
        sp = acc_p[:, lanes]
        st = active(k)
        near = sum(grid_split(st))
        at = near[0:3]
        accel = su[0:3] - at * su[6:7]
        jerk = su[3:6] - near[3:6] * su[6:7] - 3.0 * (sp[0:3] - at * sp[6:7])
        norm = jnp.sum(at * at, axis=0, keepdims=True) + soften_sq
        pot = 2.0 * jnp.sum(at * su[0:3], axis=0, keepdims=True) - su[7:8] - norm * su[6:7]
        out_ref[me ^ PARTNER[k]] = jnp.concatenate([accel, jerk, pot, jnp.zeros((1, 128), F32)], axis=0)


PARTNER = (0, 1, 2, 3, 6, 7, 4, 5)


def pair_sums(near, far, sources):
    n_act, n_src = 2 * near.shape[0], sources.shape[0]
    total = n_act * 128
    return pl.pallas_call(
        functools.partial(pair_kernel, n_src, n_act),
        out_shape=pltpu.VMEM((n_act, 8, 128), F32),
        in_specs=[pl.BlockSpec(memory_space=pltpu.VMEM)] * 3,
        out_specs=pl.BlockSpec(memory_space=pltpu.VMEM),
        scratch_shapes=[
            pltpu.VMEM((2 * n_src + 6, 8, 128), F32),
            pltpu.VMEM((256, 128), BF),
            pltpu.VMEM((n_act, 128, 128), BF),
            pltpu.VMEM((n_act, 128, 128), BF),
            pltpu.VMEM((32, 256), BF),
            pltpu.VMEM((8, total), F32),
            pltpu.VMEM((8, total), F32),
            *[pltpu.VMEM((256, 256), F32) for _ in range(2 * (total // 256))],
            *[pltpu.VMEM((4, 2, 256, 128), BF) for _ in range(total // 256)],
        ],
        name="pair_sums",
        cost_estimate=pl.CostEstimate(flops=400_000_000, bytes_accessed=400_000, transcendentals=8_000_000),
    )(*map(in_vmem, (near, far, sources)))


def pick(table, slot):
    rows = []
    for k in range(table.shape[0] // 8):
        part = table[8 * k:8 * k + 8]
        low = jnp.broadcast_to(lax.rem(slot, 128), (8, 128))
        left = jnp.take_along_axis(part[:, 0:128], low, axis=1)
        right = jnp.take_along_axis(part[:, 128:256], low, axis=1)
        rows.append(jnp.where(slot < 128, left, right))
    return jnp.concatenate(rows, axis=0)


def predict_kernel(pos_ref, vel_ref, acc_ref, jerk_ref, mass_ref, level_ref, live_ref, slot_ref, src_ref, own_ref, act_ref):
    level = level_ref[...]
    half = jnp.where((level & 1) == 1, 0.5, 1.0)
    h = 0.5 * half * jnp.where((level & 2) == 2, 0.25, 1.0)
    acc, jerk, vel = acc_ref[...], jerk_ref[...], vel_ref[...]
    pos_pred = pos_ref[...] + h * (vel + h * (acc / 2.0 + h * jerk / 6.0))
    vel_pred = vel + h * (acc + h * jerk / 2.0)
    slots = lax.broadcasted_iota(jnp.int32, (1, 256), 1)
    count = live_ref[0]
    mass = jnp.where(slots < count, mass_ref[...], 0.0)
    counts = jnp.full((1, 256), count, jnp.int32).astype(F32)
    src = jnp.concatenate([pos_pred, vel_pred, mass, counts], axis=0)
    for k in range(src_ref.shape[0]):
        src_ref[k] = src
    rest = jnp.concatenate([acc, jerk, h, h], axis=0)
    own = pick(jnp.concatenate([src, rest], axis=0), slot_ref[...])
    own_ref[...] = own
    act_ref[0] = own[0:8]


def correct_kernel(own_ref, part_ref, state_ref, deriv_ref, pot_ref):
    summed = part_ref[0]
    for k in range(1, part_ref.shape[0]):
        summed = summed + part_ref[k]
    own = own_ref[...]
    pos_now, vel_now = own[0:3], own[3:6]
    acc_start, jerk_start, step = own[8:11], own[11:14], own[14:15]
    acc_end, jerk_end = summed[0:3], summed[3:6]
    differ = acc_start - acc_end
    fourth = -6.0 * differ - step * (4.0 * jerk_start + 2.0 * jerk_end)
    fifth = 12.0 * differ + 6.0 * step * (jerk_start + jerk_end)
    new_pos = pos_now + step * step / 24.0 * fourth + step * step / 120.0 * fifth
    new_vel = vel_now + step / 6.0 * fourth + step / 24.0 * fifth
    state_ref[...] = jnp.concatenate([new_pos, new_vel], axis=0)
    deriv_ref[...] = summed[0:6]
    pot_ref[...] = summed[6:7]


VM = pl.BlockSpec(memory_space=pltpu.VMEM)
SM = pl.BlockSpec(memory_space=pltpu.SMEM)
SRC_AXES = ("y", "z")
ACT_AXES = ("x", "c")


def shards(positions, velocities, accel_old, jerk_old, masses, levels, live_count, active_slot):
    n_src = 32
    src, own, act = pl.pallas_call(
        predict_kernel,
        out_shape=(
            pltpu.VMEM((n_src, 8, 256), F32),
            pltpu.VMEM((16, 128), F32),
            pltpu.VMEM((1, 8, 128), F32),
        ),
        in_specs=[VM, VM, VM, VM, VM, VM, SM, VM],
        out_specs=(VM, VM, VM),
        name="predict",
    )(positions, velocities, accel_old, jerk_old, masses[None], levels[None], live_count, active_slot[None])
    sources = lax.all_to_all(src, SRC_AXES, 0, 0)
    two = jnp.concatenate([act, lax.ppermute(act, "c", ((0, 1), (1, 0)))])
    four = jnp.concatenate([two, lax.ppermute(two, "x", ((0, 1), (1, 0), (2, 3), (3, 2)))])
    far = lax.ppermute(four, "x", ((0, 3), (3, 0), (1, 2), (2, 1)))
    partial_sums = pair_sums(four, far, sources)
    parts = lax.all_to_all(partial_sums, ACT_AXES, 0, 0)
    state, deriv, pot = pl.pallas_call(
        correct_kernel,
        out_shape=(
            jax.ShapeDtypeStruct((6, 128), F32),
            jax.ShapeDtypeStruct((6, 128), F32),
            jax.ShapeDtypeStruct((1, 128), F32),
        ),
        in_specs=[VM, VM],
        out_specs=(VM, VM, VM),
        name="correct",
    )(in_vmem(own), in_vmem(parts))
    return state, deriv, pot[0]


def solution(mesh):
    fine = Mesh(mesh.devices.reshape(4, 4, 8, 2), ("x", "y", "z", "c"))
    every = ("x", "y", "z", "c")
    rows, flat = P(None, every), P(every)
    return jax.shard_map(
        shards,
        mesh=fine,
        in_specs=(rows, rows, rows, rows, flat, flat, flat, flat),
        out_specs=(rows, rows, flat),
        check_vma=False,
    )
```
